512 devices in a mesh: gx: 32 (over y, z_hi, core), gy: 16 (over z_lo, x).
Axes of the slice: x: 4, y: 4, z: 16 (z_hi: 4, z_lo: 4; z = z_hi * 4 + z_lo), core: 2. Of those that a mesh axis runs over, the one named last changes fastest.
Arguments:
- gradient: float32 [2, 16, 512, 2048], P(None, None, 'gx', 'gy'), may hold values from -6 to 6
- corr_length: float32 [2, 3], replicated, may hold values from 1 to 16, as said below
- scale: float32 [2, 16, 512, 2048], P(None, None, 'gx', 'gy'), may hold values from 0.25 to 4
- w_first: bfloat16 [16, 2, 3, 3, 3], replicated, may hold values from -0.875 to 0.875
- b_first: float32 [16], replicated, may hold values from -3 to 3
- w_middle: bfloat16 [16, 16, 3, 3, 3], replicated, may hold values from -0.3125 to 0.3125
- b_middle: float32 [16], replicated, may hold values from -3 to 3
- w_last: bfloat16 [2, 16, 3, 3, 3], replicated, may hold values from -0.3125 to 0.3125
- b_last: float32 [2], replicated, may hold values from -3 to 3
Outputs:
- update: float32 [2, 16, 512, 2048], P(None, None, 'gx', 'gy')
The draws below stay inside these ranges and needn't reach their ends.
Inputs may be any that keep to these rules, and one draw needn't show every extreme that they name: corr_length[:, 0] and corr_length[:, 1] lie between 6 and 16; corr_length[:, 2] lies between 1 and 2.5.
All inputs are finite; a program needn't handle non-finite values.
Results may differ from the reference program's by a relative error of at most 0.0021.
Values may be sent and summed in bfloat16 or wider, within the bound.
A program may use at most 64 MiB of HBM per device.

```python
import math
import jax
import jax.numpy as jnp
from jax import lax

FLD = 2
RAD = 16
CH = 16
NZ = 16
NX = 512
NY = 2048


def draw_corr_length(key, part):
    key_flat = jax.random.fold_in(key, 11)
    key_deep = jax.random.fold_in(key, 23)
    flat = jnp.exp(jax.random.uniform(key_flat, (FLD, 2), jnp.float32, math.log(6.0), math.log(16.0)))
    deep = jnp.exp(jax.random.uniform(key_deep, (FLD, 1), jnp.float32, math.log(1.0), math.log(2.5)))
    flat = jnp.clip(flat, 6.0, 16.0)
    deep = jnp.clip(deep, 1.0, 2.5)
    return jnp.concatenate([flat, deep], axis=1).astype(jnp.float32)


def shard_levels(stream_key, shape, pieces, low, top_value):
    gain, own = 1.0, jax.random.fold_in(stream_key, 6)
    for dim, parts in pieces:
        draws = jnp.exp(jax.random.uniform(jax.random.fold_in(own, dim), (parts,), jnp.float32, low / len(pieces), top_value / len(pieces)))
        gain = gain * jnp.repeat(draws, shape[dim] // parts).reshape([-1 if axis == dim else 1 for axis in range(len(shape))])
    return gain


def scatter_about(rng, dims, deviation, limit, shards=(), dtype=jnp.bfloat16):
    level = shard_levels(rng, dims, shards, -0.22, 0.18) if shards else 1.0
    values = jax.random.normal(rng, dims, jnp.float32) * deviation * level
    return jnp.minimum(jnp.maximum(values, -limit), limit).astype(dtype)


def setup_inputs(seed: int = 0) -> dict:
    streams_of = jax.random.split(jax.random.key(seed), 10)
    gradient = scatter_about(streams_of[0], (FLD, NZ, NX, NY), 1.0, 6.0, ((2, 32), (3, 16)), jnp.float32)
    corr_length = draw_corr_length(jax.random.fold_in(streams_of[9], 71), 0)
    scale = jnp.clip(jnp.exp(math.log(4.0) - 2.7725887 * jax.random.uniform(streams_of[2], (FLD, NZ, NX, NY), jnp.float32) ** shard_levels(streams_of[2], (FLD, NZ, NX, NY), ((2, 32), (3, 16)), -0.2, 0.2)), 0.25, 4.0)
    w_first = scatter_about(streams_of[3], (CH, FLD, 3, 3, 3), (FLD * 27) ** -0.5, 0.875)
    b_first = scatter_about(streams_of[4], (CH,), 0.5, 3.0, (), jnp.float32)
    w_middle = scatter_about(streams_of[5], (CH, CH, 3, 3, 3), (CH * 27) ** -0.5, 0.3125)
    b_middle = scatter_about(streams_of[6], (CH,), 0.5, 3.0, (), jnp.float32)
    w_last = scatter_about(streams_of[7], (FLD, CH, 3, 3, 3), (CH * 27) ** -0.5, 0.3125)
    b_last = scatter_about(streams_of[8], (FLD,), 0.5, 3.0, (), jnp.float32)
    return {"gradient": gradient, "corr_length": corr_length, "scale": scale, "w_first": w_first, "b_first": b_first, "w_middle": w_middle, "b_middle": b_middle, "w_last": w_last, "b_last": b_last}


def taps_of(length):
    reach = jnp.arange(-RAD, RAD + 1).astype(jnp.float32)
    scaled_r = math.sqrt(3.0) * jnp.abs(reach)[None, :] / length[:, None]
    values = (1.0 + scaled_r) * jnp.exp(-scaled_r)
    return values / jnp.sqrt(lax.optimization_barrier(jnp.sum(values * values, axis=1, keepdims=True)))

def smooth(padded, taps, dim):
    count = padded.shape[dim] - 2 * RAD
    total = jnp.zeros(padded.shape[:dim] + (count,) + padded.shape[dim + 1:], jnp.float32)
    for k in range(2 * RAD + 1):
        piece = lax.slice_in_dim(padded, k, k + count, axis=dim)
        total = total + taps[:, k][:, None, None, None] * piece
    return total

def convolve(field, kernel):
    return lax.conv_general_dilated(field[None], kernel, (1, 1, 1), ((1, 1), (0, 0), (0, 0)), dimension_numbers=('NCDHW', 'OIDHW', 'NCDHW'), preferred_element_type=jnp.float32)[0]

def domain_mask(field, row_first, rim, rows_all, cols_all):
    rows = row_first - rim + jnp.arange(field.shape[2])
    cols = -rim + jnp.arange(field.shape[3])
    keep_rows = (rows >= 0) & (rows < rows_all)
    keep_cols = (cols >= 0) & (cols < cols_all)
    keep = keep_rows[:, None] & keep_cols[None, :]
    return jnp.where(keep[None, None], field, jnp.zeros_like(field))

def reference(gradient, corr_length, scale, w_first, b_first, w_middle, b_middle, w_last, b_last):
    taps_x = taps_of(corr_length[:, 0])
    taps_y = taps_of(corr_length[:, 1])
    taps_z = taps_of(corr_length[:, 2])
    along_x = smooth(jnp.pad(gradient, ((0, 0), (0, 0), (RAD, RAD), (0, 0))), taps_x, 2)
    along_y = smooth(jnp.pad(along_x, ((0, 0), (0, 0), (0, 0), (RAD, RAD))), taps_y, 3)
    smoothed = smooth(jnp.pad(along_y, ((0, 0), (RAD, RAD), (0, 0), (0, 0))), taps_z, 1)
    scaled = scale * smoothed
    net_in = scaled.astype(jnp.bfloat16)
    padded_in = jnp.pad(net_in, ((0, 0), (0, 0), (3, 3), (3, 3)))
    block = math.gcd(NX, 64)

    def one_block(index):
        start = (index * block).astype(jnp.int32)
        piece = lax.dynamic_slice_in_dim(padded_in, start, block + 6, 2)
        hidden = jax.nn.silu(convolve(piece, w_first) + b_first[:, None, None, None]).astype(jnp.bfloat16)
        hidden = domain_mask(hidden, start, 2, NX, NY)
        hidden = jax.nn.silu(convolve(hidden, w_middle) + b_middle[:, None, None, None]).astype(jnp.bfloat16)
        hidden = domain_mask(hidden, start, 1, NX, NY)
        return convolve(hidden, w_last) + b_last[:, None, None, None]
    blocks = lax.map(one_block, jnp.arange(NX // block).astype(jnp.int32))
    correction = jnp.moveaxis(blocks, 0, 2).reshape(FLD, NZ, NX, NY)
    return scaled + correction
```

```python
import math

import jax
import jax.numpy as jnp
from jax import lax
from jax.experimental import pallas as pl
from jax.experimental.pallas import tpu as pltpu
from jax.sharding import PartitionSpec as P

RAD = 16
RIM = 3
HALO = RAD + RIM
MESH = pl.DeviceIdType.MESH
F32 = jnp.float32
BF16 = jnp.bfloat16
ROWS = 144
ROOT = math.sqrt(3.0)


def iota(shape, dim):
    return lax.broadcasted_iota(jnp.int32, shape, dim)


def dot(a, b):
    return lax.dot_general(a, b, (((1,), (0,)), ((), ())), preferred_element_type=F32)


def split(value):
    high = value.astype(BF16)
    return high, (value - high.astype(F32)).astype(BF16)


def tap(length, distance):
    s = (ROOT * distance.astype(F32)) / length
    return (1.0 + s) * jnp.exp(-s)


def tap_rows(length):
    rows = [tap(length, jnp.full((8, 128), r, jnp.int32)) for r in range(RAD + 1)]
    total = rows[0] * rows[0]
    for row in rows[1:]:
        total = total + 2.0 * (row * row)
    inverse = 1.0 / jnp.sqrt(total)
    return [row * inverse for row in rows], inverse


def silu(v):
    return v / (1.0 + jnp.exp(-v))


def kernel(
    nx, ny, lens, b1s, b2s, b3s, g_ref, s_ref, w1, w2, w3, out_ref,
    gsend, ssend, xl, xr, sl, sr, field, along, scales, pack_l, pack_r, from_l, from_r,
    own_h, own_l, rim_h, rim_l, zmat, smooth, rimscale, scaled, turned, lhs, hid1, hid2, t1, t2, t3,
    send_sem, recv_sem, ysend_sem, yrecv_sem,
):
    gx = lax.axis_index("gx")
    gy = lax.axis_index("gy")
    at = lambda step: {"gx": lax.rem(gx + nx + step, nx)}

    for x in range(16):
        gsend[x] = g_ref[pl.ds(x, 32, stride=16), :].reshape(2, 16, 128).astype(BF16)
    for n, x in enumerate((0, 1, 2, 13, 14, 15)):
        ssend[n] = s_ref[pl.ds(x, 32, stride=16), :].reshape(2, 16, 128).astype(BF16)

    barrier = pltpu.get_barrier_semaphore()
    for step in (-1, 1, -2, 2):
        pl.semaphore_signal(barrier, inc=1, device_id=at(step), device_id_type=MESH)

    for step in (1, ny - 1):
        pl.semaphore_signal(barrier, inc=1, device_id={"gy": lax.rem(gy + step, ny)}, device_id_type=MESH)
    pl.semaphore_wait(barrier, 6)

    def remote(src, dst, n, step):
        return pltpu.make_async_remote_copy(
            src_ref=src, dst_ref=dst, send_sem=send_sem.at[n], recv_sem=recv_sem.at[n],
            device_id=at(step), device_id_type=MESH,
        )

    copies = [
        remote(gsend, xl.at[pl.ds(RIM, 16)], 0, 1),
        remote(gsend, xr.at[pl.ds(0, 16)], 1, -1),
        remote(gsend.at[pl.ds(13, 3)], xl.at[pl.ds(0, RIM)], 2, 2),
        remote(gsend.at[pl.ds(0, 3)], xr.at[pl.ds(16, RIM)], 3, -2),
        remote(ssend.at[pl.ds(3, 3)], sl, 4, 1),
        remote(ssend.at[pl.ds(0, 3)], sr, 5, -1),
    ]
    for copy in copies:
        copy.start()

    for x in range(16):
        field[HALO + x] = g_ref[pl.ds(x, 32, stride=16), :].reshape(4, 8, 128)
        scales[RIM + x] = s_ref[pl.ds(x, 32, stride=16), :]
    for x in (22, 23):
        scales[x] = jnp.zeros((32, 128), F32)
        along[x] = jnp.zeros((4, 8, 128), F32)

    pick = (iota((16, 256), 1) % 16 == iota((16, 256), 0)).astype(BF16)
    level = iota((16, 256), 1) // 16
    wide1 = dot(w1[...], pick)
    row = iota((16, 256), 0)
    for dy in range(3):
        for dx in range(3):
            for f in range(2):
                block = jnp.zeros((16, 256), F32)
                for dz in range(3):
                    k = ((dx * 3 + dy) * 3 + dz) * 2 + f
                    block = jnp.where(level == row + 1 - dz, wide1[k : k + 1, :], block)
                t1[dy * 128 + dx * 32 + f * 16 : dy * 128 + dx * 32 + f * 16 + 16, :] = block.astype(BF16)
        t1[dy * 128 + 96 : dy * 128 + 128, :] = jnp.zeros((32, 256), BF16)

    def one_pair(n, carry):
        blocks = [dot(w2[pl.ds(n * 48 + dz * 16, 16), :], pick) for dz in range(3)]
        for zi in range(16):
            block = jnp.zeros((16, 256), F32)
            for dz in range(3):
                block = jnp.where(level == zi + 1 - dz, blocks[dz], block)
            t2[n, zi * 16 : zi * 16 + 16, :] = block.astype(BF16)
        return carry

    lax.fori_loop(0, 9, one_pair, 0)

    lane = iota((16, 128), 1)
    pick3 = ((iota((8, 128), 1) // 16 == iota((8, 128), 0)) & (iota((8, 128), 0) < 6)).astype(BF16)

    def one_shift(dx, carry):
        blocks = [dot(w3[pl.ds(dx * 48 + dz * 16, 16), :], pick3) for dz in range(3)]
        for zi in range(16):
            block = jnp.zeros((16, 128), F32)
            for dz in range(3):
                block = jnp.where((lane % 16 == zi + 1 - dz) & (lane < 96), blocks[dz], block)
            t3[dx, zi * 16 : zi * 16 + 16, :] = block.astype(BF16)
        return carry

    lax.fori_loop(0, 3, one_shift, 0)

    for f in range(2):
        length = lens[f, 1]
        inverse = tap_rows(length)[1][0:1, :]
        inverse2 = jnp.concatenate([inverse, inverse], axis=1)
        lanes = iota((128, 256), 1)
        target = jnp.where(lanes < 128, lanes, jnp.where(lanes < 131, lanes - 131, lanes - 3))
        away = jnp.abs(iota((128, 256), 0) - target)
        band = jnp.where((away <= RAD) & (lanes < 134), tap(length, away) * inverse2, 0.0)
        own_h[f], own_l[f] = split(band)

        def one_quarter(j, carry):
            for side in range(2):
                place = iota((128, 256), 0)
                k = place % 32
                source = k - HALO if side == 0 else k + 128
                away = jnp.abs(source - target)
                good = (place // 32 == j) & (k < HALO) & (away <= RAD) & (lanes < 134)
                band = jnp.where(good, tap(length, away) * inverse2, 0.0)
                high, low = split(band)
                rim_h[f, j, side * 128 : side * 128 + 128, 0:256] = high
                rim_l[f, j, side * 128 : side * 128 + 128, 0:256] = low
                place1 = iota((128, 128), 0)
                one = (place1 // 32 == j) & (place1 % 32 >= HALO) & (place1 % 32 < HALO + RIM)
                one = one & (iota((128, 128), 1) == place1 % 32 - HALO + RIM * side)
                rim_h[f, j, side * 128 : side * 128 + 128, 256:384] = one.astype(BF16)
                rim_l[f, j, side * 128 : side * 128 + 128, 256:384] = jnp.zeros((128, 128), BF16)
            return carry

        lax.fori_loop(0, 4, one_quarter, 0)

    inv0 = tap_rows(lens[0, 2])[1][0:1, 0:32]
    inv1 = tap_rows(lens[1, 2])[1][0:1, 0:32]
    zo = iota((32, 32), 0)
    zi = iota((32, 32), 1)
    away = jnp.abs(zo - zi)
    both = jnp.where(zo < 16, tap(lens[0, 2], away) * inv0, tap(lens[1, 2], away) * inv1)
    z_high, z_low = split(jnp.where(zo // 16 == zi // 16, both, 0.0))
    zmat[...] = jnp.concatenate([z_high, z_high, z_low], axis=1)

    for copy in copies:
        copy.wait()

    for x in range(HALO):
        left_in = gx * 16 - HALO + x >= 0
        right_in = gx * 16 + 16 + x < nx * 16
        field[x] = jnp.where(left_in, xl[x].astype(F32), 0.0).reshape(4, 8, 128)
        field[HALO + 16 + x] = jnp.where(right_in, xr[x].astype(F32), 0.0).reshape(4, 8, 128)
    for x in range(RIM):
        scales[x] = jnp.where(gx > 0, sl[x].astype(F32), 0.0).reshape(32, 128)
        scales[RIM + 16 + x] = jnp.where(gx < nx - 1, sr[x].astype(F32), 0.0).reshape(32, 128)

    for f in range(2):
        rows = tap_rows(lens[f, 0])[0]

        def one_x(x, carry):
            part = lambda k: field[x + k, 2 * f : 2 * f + 2]
            total = rows[0] * part(RAD)
            for r in range(1, RAD + 1):
                total = total + rows[r] * (part(RAD - r) + part(RAD + r))
            along[x, 2 * f : 2 * f + 2] = total
            return carry

        lax.fori_loop(0, 22, one_x, 0)

    lane32 = iota((32, 128), 1)

    def one_group(g, carry):
        left = jnp.zeros((32, 128), F32)
        right = jnp.zeros((32, 128), F32)
        for j in range(4):
            a = along[4 * g + j].reshape(32, 128)
            s = scales[4 * g + j]
            inside = (lane32 >= 32 * j) & (lane32 < 32 * j + HALO)
            beside = (lane32 >= 32 * j + HALO) & (lane32 < 32 * j + HALO + RIM)
            right = jnp.where(inside, pltpu.roll(a, (32 * j + HALO) % 128, 1), right)
            right = jnp.where(beside, pltpu.roll(s, (32 * j + HALO + RIM) % 128, 1), right)
            left = jnp.where(inside, a if j == 0 else pltpu.roll(a, 32 * j, 1), left)
            left = jnp.where(beside, pltpu.roll(s, 32 * j + HALO, 1), left)
        pack_l[g] = left
        pack_r[g] = right
        return carry

    lax.fori_loop(0, 6, one_group, 0)

    def edge(src, dst, n, to):
        return pltpu.make_async_remote_copy(
            src_ref=src, dst_ref=dst, send_sem=ysend_sem.at[n], recv_sem=yrecv_sem.at[n],
            device_id={"gy": to}, device_id_type=MESH,
        )

    to_right = edge(pack_r, from_l, 0, lax.rem(gy + 1, ny))
    to_left = edge(pack_l, from_r, 1, lax.rem(gy + ny - 1, ny))

    @pl.when(gy < ny - 1)
    def _():
        to_right.start()

    @pl.when(gy > 0)
    def _():
        to_left.start()

    for f in range(2):
        high, low = split(along[:, 2 * f : 2 * f + 2].reshape(384, 128))
        own = dot(high, own_h[f]) + dot(low, own_h[f]) + dot(high, own_l[f])
        smooth[:, f * 16 : f * 16 + 16, :] = own.reshape(24, 16, 256)

    @pl.when(gy < ny - 1)
    def _():
        to_right.wait_send()
        to_left.wait_recv()

    @pl.when(gy > 0)
    def _():
        to_left.wait_send()
        to_right.wait_recv()

    edge_l = jnp.where(gy > 0, from_l[...], 0.0)
    edge_r = jnp.where(gy < ny - 1, from_r[...], 0.0)
    for f in range(2):
        a = jnp.concatenate(
            [edge_l[:, f * 16 : f * 16 + 16].reshape(96, 128), edge_r[:, f * 16 : f * 16 + 16].reshape(96, 128)], axis=1
        )
        high, low = split(a)
        for j in range(4):
            rim = dot(high, rim_h[f, j]) + dot(low, rim_h[f, j]) + dot(high, rim_l[f, j])
            rim = rim.reshape(6, 16, 384)
            for g in range(6):
                x = 4 * g + j
                smooth[x, f * 16 : f * 16 + 16, :] += rim[g, :, 0:256]
                rimscale[x, f * 16 : f * 16 + 16, :] = rim[g, :, 256:384]

    def one_z(x, carry):
        high, low = split(smooth[x])
        z = dot(zmat[...], jnp.concatenate([high, low, high], axis=0))
        scaled[x, :, 0:128] = z[:, 0:128] * scales[x]
        scaled[x, :, 128:256] = z[:, 128:256] * rimscale[x]
        return carry

    lax.fori_loop(0, 24, one_z, 0)

    def one_turn(x, carry):
        turned[16:144, :] = scaled[pl.ds(x, 4), :, 0:128].reshape(128, 128).T
        rim = scaled[pl.ds(x, 4), :, 128:256].reshape(128, 128).T
        turned[13:16, :] = rim[0:3]
        turned[144:147, :] = rim[3:6]
        for dy in range(3):
            lhs[x, :, dy * 128 : dy * 128 + 128] = turned[7 + dy : 7 + dy + ROWS, :].astype(BF16)
        return carry

    turned[0:16, :] = jnp.zeros((16, 128), F32)
    turned[144:160, :] = jnp.zeros((16, 128), F32)
    lax.fori_loop(0, 20, one_turn, 0)

    lane256 = iota((1, 256), 1) % 16
    bias1 = jnp.zeros((1, 256), F32)
    bias2 = jnp.zeros((1, 256), F32)
    for o in range(16):
        bias1 = jnp.where(lane256 == o, b1s[o], bias1)
        bias2 = jnp.where(lane256 == o, b2s[o], bias2)
    y = iota((ROWS, 256), 0) - 8 + gy * 128
    y_in = (y >= 0) & (y < ny * 128)

    def one_first(c, carry):
        v = dot(lhs[pl.ds(c * 4, 4)].reshape(4 * ROWS, 384), t1[...]) + bias1
        v = silu(v).reshape(4, ROWS, 256)
        for n in range(4):
            x = gx * 16 - 2 + c * 4 + n
            h = jnp.where(y_in & (x >= 0) & (x < nx * 16), v[n], 0.0)
            hid1[c * 4 + n, :, 0:256] = pltpu.roll(h, 1, 0).astype(BF16)
            hid1[c * 4 + n, :, 256:512] = h.astype(BF16)
            hid1[c * 4 + n, :, 512:768] = pltpu.roll(h, ROWS - 1, 0).astype(BF16)
        return carry

    lax.fori_loop(0, 5, one_first, 0)

    def one_middle(c, carry):
        v = bias2
        for dx in range(3):
            v = v + dot(hid1[pl.ds(c * 6 + dx, 6)].reshape(6 * ROWS, 768), t2[pl.ds(3 * dx, 3)].reshape(768, 256))
        v = silu(v).reshape(6, ROWS, 256)
        for n in range(6):
            x = gx * 16 - 1 + c * 6 + n
            hid2[c * 6 + n] = jnp.where(y_in & (x >= 0) & (x < nx * 16), v[n], 0.0).astype(BF16)
        return carry

    lax.fori_loop(0, 3, one_middle, 0)

    lane3 = iota((ROWS, 128), 1)
    bias3 = jnp.where(iota((32, 128), 0) < 16, b3s[0], b3s[1])
    for c in range(4):
        p = dot(hid2[c * 4 : c * 4 + 4].reshape(4 * ROWS, 256), t3[0])
        for dx in range(1, 3):
            p = p + dot(hid2[c * 4 + dx : c * 4 + dx + 4].reshape(4 * ROWS, 256), t3[dx])
        p = p.reshape(4, ROWS, 128)
        for n in range(4):
            x = c * 4 + n
            q = jnp.where(lane3 < 32, pltpu.roll(p[n], 1, 0), jnp.where(lane3 < 64, p[n], pltpu.roll(p[n], ROWS - 1, 0)))
            q = q[8:136].T
            total = q[0:32] + q[32:64] + q[64:96] + bias3 + scaled[x + RIM, :, 0:128]
            out_ref[pl.ds(x, 32, stride=16), :] = total


def solution(mesh):
    nx, ny = mesh.shape["gx"], mesh.shape["gy"]

    def per_device(gradient, corr_length, scale, w_first, b_first, w_middle, b_middle, w_last, b_last):
        w1 = jnp.transpose(w_first, (3, 4, 2, 1, 0)).reshape(54, 16)
        w1 = jnp.pad(w1, ((0, 10), (0, 0)))
        w2 = jnp.transpose(w_middle, (3, 4, 2, 1, 0)).reshape(432, 16)
        w3 = jnp.transpose(w_last, (3, 2, 1, 4, 0)).reshape(144, 6)
        w3 = jnp.pad(w3, ((0, 0), (0, 2)))
        smem = pl.BlockSpec(memory_space=pltpu.SMEM)
        vmem = pl.BlockSpec(memory_space=pltpu.VMEM)

        def body(*refs):
            kernel(nx, ny, *refs)

        v = pltpu.VMEM
        out = pl.pallas_call(
            body,
            out_shape=jax.ShapeDtypeStruct((512, 128), F32),
            in_specs=[smem] * 4 + [vmem] * 5,
            out_specs=vmem,
            scratch_shapes=[
                v((16, 2, 16, 128), BF16), v((6, 2, 16, 128), BF16),
                v((HALO, 2, 16, 128), BF16), v((HALO, 2, 16, 128), BF16),
                v((RIM, 2, 16, 128), BF16), v((RIM, 2, 16, 128), BF16),
                v((54, 4, 8, 128), F32), v((24, 4, 8, 128), F32), v((24, 32, 128), F32),
                v((6, 32, 128), F32), v((6, 32, 128), F32), v((6, 32, 128), F32), v((6, 32, 128), F32),
                v((2, 128, 256), BF16), v((2, 128, 256), BF16),
                v((2, 4, 256, 384), BF16), v((2, 4, 256, 384), BF16), v((32, 96), BF16),
                v((24, 32, 256), F32), v((24, 32, 128), F32), v((24, 32, 256), F32),
                v((160, 128), F32), v((20, ROWS, 384), BF16), v((20, ROWS, 768), BF16), v((18, ROWS, 256), BF16),
                v((384, 256), BF16), v((9, 256, 256), BF16), v((3, 256, 128), BF16),
                pltpu.SemaphoreType.DMA((6,)), pltpu.SemaphoreType.DMA((6,)),
                pltpu.SemaphoreType.DMA((2,)), pltpu.SemaphoreType.DMA((2,)),
            ],
            compiler_params=pltpu.CompilerParams(
                collective_id=0, has_side_effects=True, vmem_limit_bytes=56 * 1024 * 1024
            ),
        )(corr_length, b_first, b_middle, b_last, gradient.reshape(512, 128), scale.reshape(512, 128), w1, w2, w3)
        return out.reshape(gradient.shape)

    block = P(None, None, "gx", "gy")
    return jax.shard_map(
        per_device,
        mesh=mesh,
        in_specs=(block, P(), block, P(), P(), P(), P(), P(), P()),
        out_specs=block,
        check_vma=False,
    )
```

```python
import math

import jax
import jax.numpy as jnp
from jax import lax
from jax.experimental import pallas as pl
from jax.experimental.pallas import tpu as pltpu
from jax.sharding import PartitionSpec as P

RAD = 16
RIM = 3
HALO = RAD + RIM
MESH = pl.DeviceIdType.MESH
F32 = jnp.float32
BF16 = jnp.bfloat16
ROWS = 144
ROOT = math.sqrt(3.0)


def iota(shape, dim):
    return lax.broadcasted_iota(jnp.int32, shape, dim)


def dot(a, b):
    return lax.dot_general(a, b, (((1,), (0,)), ((), ())), preferred_element_type=F32)


def dot_rows(a, b):
    return lax.dot_general(a, b, (((0,), (0,)), ((), ())), preferred_element_type=F32)


def split(value):
    high = value.astype(BF16)
    return high, (value - high.astype(F32)).astype(BF16)


def tap(length, distance):
    s = (ROOT * distance.astype(F32)) / length
    return (1.0 + s) * jnp.exp(-s)


def tap_rows(length):
    rows = [tap(length, jnp.full((8, 128), r, jnp.int32)) for r in range(RAD + 1)]
    total = rows[0] * rows[0]
    for row in rows[1:]:
        total = total + 2.0 * (row * row)
    inverse = 1.0 / jnp.sqrt(total)
    return [row * inverse for row in rows], inverse


def silu(v):
    return v / (1.0 + jnp.exp(-v))


def kernel(
    nx, ny, lens, b1s, b2s, b3s, g_ref, s_ref, w1, w2, w3, out_ref,
    gsend, ssend, xl, xr, sl, sr, field, along, scales, pack_l, pack_r, from_l, from_r,
    own_h, own_l, rim_h, rim_l, zmat, smooth, scaled, turned, lhs, hid1, hid2, t1, t2, t3, flat1, flat3,
    send_sem, recv_sem, ysend_sem, yrecv_sem,
):
    gx = lax.axis_index("gx")
    gy = lax.axis_index("gy")
    at = lambda step: {"gx": lax.rem(gx + nx + step, nx)}

    for f in range(2):
        for x in range(16):
            gsend[f, x] = g_ref[pl.ds(f * 256 + x, 16, stride=16), :].astype(BF16)
        for n, x in enumerate((0, 1, 2, 13, 14, 15)):
            ssend[f, n] = s_ref[pl.ds(f * 256 + x, 16, stride=16), :].astype(BF16)

    barrier = pltpu.get_barrier_semaphore()
    for step in (-1, 1, -2, 2):
        pl.semaphore_signal(barrier, inc=1, device_id=at(step), device_id_type=MESH)

    for step in (1, ny - 1):
        pl.semaphore_signal(barrier, inc=1, device_id={"gy": lax.rem(gy + step, ny)}, device_id_type=MESH)
    pl.semaphore_wait(barrier, 6)

    def remote(src, dst, n, step):
        return pltpu.make_async_remote_copy(
            src_ref=src, dst_ref=dst, send_sem=send_sem.at[n], recv_sem=recv_sem.at[n],
            device_id=at(step), device_id_type=MESH,
        )

    copies = []
    for f in range(2):
        n = 6 * f
        copies.append([
            remote(gsend.at[f], xl.at[f, pl.ds(RIM, 16)], n, 1),
            remote(gsend.at[f], xr.at[f, pl.ds(0, 16)], n + 1, -1),
            remote(gsend.at[f, pl.ds(13, 3)], xl.at[f, pl.ds(0, RIM)], n + 2, 2),
            remote(gsend.at[f, pl.ds(0, 3)], xr.at[f, pl.ds(16, RIM)], n + 3, -2),
            remote(ssend.at[f, pl.ds(3, 3)], sl.at[f], n + 4, 1),
            remote(ssend.at[f, pl.ds(0, 3)], sr.at[f], n + 5, -1),
        ])
    for copy in copies[0] + copies[1]:
        copy.start()

    for x in range(16):
        field[HALO + x] = g_ref[pl.ds(x, 32, stride=16), :].reshape(4, 8, 128)
        scales[RIM + x] = s_ref[pl.ds(x, 32, stride=16), :]
    for x in (22, 23):
        scales[x] = jnp.zeros((32, 128), F32)
        along[x] = jnp.zeros((4, 8, 128), F32)
        scaled[x] = jnp.zeros((32, 256), F32)

    for x in range(20):
        turned[x, 0:16, :] = jnp.zeros((16, 128), F32)
        turned[x, 144:160, :] = jnp.zeros((16, 128), F32)

    pick = (iota((16, 256), 1) % 16 == iota((16, 256), 0)).astype(BF16)
    level = iota((16, 256), 1) // 16
    flat3[...] = jnp.zeros((72, 16), F32)
    for k in range(27):
        flat1[2 * k : 2 * k + 2, :] = w1[k].astype(F32)
        flat3[k // 3 * 8 + k % 3 * 2 : k // 3 * 8 + k % 3 * 2 + 2, :] = w3[k].astype(F32)
    wide1 = dot(flat1[...].astype(BF16), pick)
    row = iota((16, 256), 0)
    for dy in range(3):
        for dx in range(3):
            for f in range(2):
                block = jnp.zeros((16, 256), F32)
                for dz in range(3):
                    k = ((dz * 3 + dx) * 3 + dy) * 2 + f
                    block = jnp.where(level == row + 1 - dz, wide1[k : k + 1, :], block)
                t1[dy * 128 + dx * 32 + f * 16 : dy * 128 + dx * 32 + f * 16 + 16, :] = block.astype(BF16)
        t1[dy * 128 + 96 : dy * 128 + 128, :] = jnp.zeros((32, 256), BF16)

    def one_pair(n, carry):
        blocks = [dot_rows(w2[pl.ds(pl.multiple_of((dz * 9 + n) * 16, 16), 16), :], pick) for dz in range(3)]
        for zi in range(16):
            block = jnp.zeros((16, 256), F32)
            for dz in range(3):
                block = jnp.where(level == zi + 1 - dz, blocks[dz], block)
            t2[n, zi * 16 : zi * 16 + 16, :] = block.astype(BF16)
        return carry

    lax.fori_loop(0, 9, one_pair, 0)

    lane = iota((16, 128), 1)
    pick3 = ((iota((8, 128), 1) // 16 == iota((8, 128), 0)) & (iota((8, 128), 0) < 6)).astype(BF16)

    def one_shift(dx, carry):
        blocks = [dot_rows(flat3[pl.ds(pl.multiple_of((dz * 3 + dx) * 8, 8), 8), :].astype(BF16), pick3) for dz in range(3)]
        for zi in range(16):
            block = jnp.zeros((16, 128), F32)
            for dz in range(3):
                block = jnp.where((lane % 16 == zi + 1 - dz) & (lane < 96), blocks[dz], block)
            t3[dx, zi * 16 : zi * 16 + 16, :] = block.astype(BF16)
        return carry

    lax.fori_loop(0, 3, one_shift, 0)

    for f in range(2):
        length = lens[f, 1]
        inverse = tap_rows(length)[1][0:1, :]
        inverse2 = jnp.concatenate([inverse, inverse], axis=1)
        lanes = iota((128, 256), 1)
        target = jnp.where(lanes < 128, lanes, jnp.where(lanes < 131, lanes - 131, lanes - 3))
        away = jnp.abs(iota((128, 256), 0) - target)
        band = jnp.where((away <= RAD) & (lanes < 134), tap(length, away) * inverse2, 0.0)
        own_h[f], own_l[f] = split(band)

        def one_quarter(j, carry):
            for side in range(2):
                place = iota((128, 256), 0)
                k = place % 32
                source = k - HALO if side == 0 else k + 128
                away = jnp.abs(source - target)
                good = (place // 32 == j) & (k < HALO) & (away <= RAD) & (lanes < 134)
                band = jnp.where(good, tap(length, away) * inverse2, 0.0)
                high, low = split(band)
                rim_h[f, j, side * 128 : side * 128 + 128, 0:256] = high
                rim_l[f, j, side * 128 : side * 128 + 128, 0:256] = low
                place1 = iota((128, 128), 0)
                one = (place1 // 32 == j) & (place1 % 32 >= HALO) & (place1 % 32 < HALO + RIM)
                one = one & (iota((128, 128), 1) == place1 % 32 - HALO + RIM * side)
                rim_h[f, j, side * 128 : side * 128 + 128, 256:384] = one.astype(BF16)
                rim_l[f, j, side * 128 : side * 128 + 128, 256:384] = jnp.zeros((128, 128), BF16)
            return carry

        lax.fori_loop(0, 4, one_quarter, 0)

    away = jnp.abs(iota((16, 16), 0) - iota((16, 16), 1))
    for f in range(2):
        inverse = tap_rows(lens[f, 2])[1][0:1, 0:16]
        high, low = split(tap(lens[f, 2], away) * inverse)
        zmat[f] = jnp.concatenate([high, high, low], axis=1)

    def weighted(rows, f, x, kept):
        part = lambda k: field[x + k, 2 * f : 2 * f + 2]
        total = None
        for r in range(RAD + 1):
            taken = [part(k) for k in sorted({RAD - r, RAD + r}) if kept(x + k)]
            if taken:
                term = rows[r] * (taken[0] if len(taken) == 1 else taken[0] + taken[1])
                total = term if total is None else total + term
        return total

    mine = lambda row: HALO <= row < HALO + 16
    for f in range(2):
        rows = tap_rows(lens[f, 0])[0]
        for x in range(22):
            along[x, 2 * f : 2 * f + 2] = weighted(rows, f, x, mine)

    lane16 = iota((16, 128), 1)

    def edge(src, dst, n, to):
        return pltpu.make_async_remote_copy(
            src_ref=src, dst_ref=dst, send_sem=ysend_sem.at[n], recv_sem=yrecv_sem.at[n],
            device_id={"gy": to}, device_id_type=MESH,
        )

    to_right = [edge(pack_r.at[f], from_l.at[f], f, lax.rem(gy + 1, ny)) for f in range(2)]
    to_left = [edge(pack_l.at[f], from_r.at[f], 2 + f, lax.rem(gy + ny - 1, ny)) for f in range(2)]

    for f in range(2):
        for copy in copies[f]:
            copy.wait()
        for x in range(HALO):
            left_in = gx * 16 - HALO + x >= 0
            right_in = gx * 16 + 16 + x < nx * 16
            field[x, 2 * f : 2 * f + 2] = jnp.where(left_in, xl[f, x].astype(F32), 0.0).reshape(2, 8, 128)
            field[HALO + 16 + x, 2 * f : 2 * f + 2] = jnp.where(right_in, xr[f, x].astype(F32), 0.0).reshape(2, 8, 128)
        for x in range(RIM):
            scales[x, 16 * f : 16 * f + 16] = jnp.where(gx > 0, sl[f, x].astype(F32), 0.0)
            scales[RIM + 16 + x, 16 * f : 16 * f + 16] = jnp.where(gx < nx - 1, sr[f, x].astype(F32), 0.0)
        rows = tap_rows(lens[f, 0])[0]
        for x in range(22):
            along[x, 2 * f : 2 * f + 2] += weighted(rows, f, x, lambda row: not mine(row))

        for g in range(6):
            left = jnp.zeros((16, 128), F32)
            right = jnp.zeros((16, 128), F32)
            for j in range(4):
                a = along[4 * g + j, 2 * f : 2 * f + 2].reshape(16, 128)
                s = scales[4 * g + j, 16 * f : 16 * f + 16]
                inside = (lane16 >= 32 * j) & (lane16 < 32 * j + HALO)
                beside = (lane16 >= 32 * j + HALO) & (lane16 < 32 * j + HALO + RIM)
                right = jnp.where(inside, pltpu.roll(a, (32 * j + HALO) % 128, 1), right)
                right = jnp.where(beside, pltpu.roll(s, (32 * j + HALO + RIM) % 128, 1), right)
                left = jnp.where(inside, a if j == 0 else pltpu.roll(a, 32 * j, 1), left)
                left = jnp.where(beside, pltpu.roll(s, 32 * j + HALO, 1), left)
            pack_l[f, g] = left
            pack_r[f, g] = right

        @pl.when(gy < ny - 1)
        def _():
            to_right[f].start()

        @pl.when(gy > 0)
        def _():
            to_left[f].start()

        high, low = split(along[:, 2 * f : 2 * f + 2].reshape(384, 128))
        own = dot(high, own_h[f]) + dot(low, own_h[f]) + dot(high, own_l[f])
        smooth[:, f * 16 : f * 16 + 16, :] = own.reshape(24, 16, 256)

    for f in range(2):
        @pl.when(gy < ny - 1)
        def _():
            to_right[f].wait_send()
            to_left[f].wait_recv()

        @pl.when(gy > 0)
        def _():
            to_left[f].wait_send()
            to_right[f].wait_recv()

        edge_l = jnp.where(gy > 0, from_l[f], 0.0).reshape(96, 128)
        edge_r = jnp.where(gy < ny - 1, from_r[f], 0.0).reshape(96, 128)
        high, low = split(jnp.concatenate([edge_l, edge_r], axis=1))
        for j in range(4):
            rim = dot(high, rim_h[f, j]) + dot(low, rim_h[f, j]) + dot(high, rim_l[f, j])
            rim = rim.reshape(6, 16, 384)
            for g in range(6):
                x = 4 * g + j
                if x < 22:
                    part = slice(f * 16, f * 16 + 16)
                    high1, low1 = split(smooth[x, part, :] + rim[g, :, 0:256])
                    z = dot(zmat[f], jnp.concatenate([high1, low1, high1], axis=0))
                    scaled[x, part, 0:128] = z[:, 0:128] * scales[x, part]
                    scaled[x, part, 128:256] = z[:, 128:256] * rim[g, :, 256:384]

    def one_turn(x, carry):
        turned[x, 16:144, :] = scaled[pl.ds(x, 4), :, 0:128].reshape(128, 128).T
        rim = scaled[pl.ds(x, 4), :, 128:256].reshape(128, 128).T
        turned[x, 13:16, :] = rim[0:3]
        turned[x, 144:147, :] = rim[3:6]
        for dy in range(3):
            lhs[x, :, dy * 128 : dy * 128 + 128] = turned[x, 7 + dy : 7 + dy + ROWS, :].astype(BF16)
        return carry

    lax.fori_loop(0, 20, one_turn, 0, unroll=5)

    lane256 = iota((1, 256), 1) % 16
    bias1 = jnp.zeros((1, 256), F32)
    bias2 = jnp.zeros((1, 256), F32)
    for o in range(16):
        bias1 = jnp.where(lane256 == o, b1s[o], bias1)
        bias2 = jnp.where(lane256 == o, b2s[o], bias2)
    y = iota((ROWS, 256), 0) - 8 + gy * 128
    y_in = (y >= 0) & (y < ny * 128)

    def one_first(c, carry):
        v = dot(lhs[pl.ds(c * 4, 4)].reshape(4 * ROWS, 384), t1[...]) + bias1
        v = silu(v).reshape(4, ROWS, 256)
        for n in range(4):
            x = gx * 16 - 2 + c * 4 + n
            h = jnp.where(y_in & (x >= 0) & (x < nx * 16), v[n], 0.0)
            hid1[c * 4 + n, :, 0:256] = pltpu.roll(h, 1, 0).astype(BF16)
            hid1[c * 4 + n, :, 256:512] = h.astype(BF16)
            hid1[c * 4 + n, :, 512:768] = pltpu.roll(h, ROWS - 1, 0).astype(BF16)
        return carry

    lax.fori_loop(0, 5, one_first, 0)

    def one_middle(c, carry):
        v = bias2
        for dx in range(3):
            v = v + dot(hid1[pl.ds(c * 6 + dx, 6)].reshape(6 * ROWS, 768), t2[pl.ds(3 * dx, 3)].reshape(768, 256))
        v = silu(v).reshape(6, ROWS, 256)
        for n in range(6):
            x = gx * 16 - 1 + c * 6 + n
            hid2[c * 6 + n] = jnp.where(y_in & (x >= 0) & (x < nx * 16), v[n], 0.0).astype(BF16)
        return carry

    lax.fori_loop(0, 3, one_middle, 0)

    lane3 = iota((ROWS, 128), 1)
    bias3 = jnp.where(iota((32, 128), 0) < 16, b3s[0], b3s[1])
    for c in range(4):
        p = dot(hid2[c * 4 : c * 4 + 4].reshape(4 * ROWS, 256), t3[0])
        for dx in range(1, 3):
            p = p + dot(hid2[c * 4 + dx : c * 4 + dx + 4].reshape(4 * ROWS, 256), t3[dx])
        p = p.reshape(4, ROWS, 128)
        for n in range(4):
            x = c * 4 + n
            q = jnp.where(lane3 < 32, pltpu.roll(p[n], 1, 0), jnp.where(lane3 < 64, p[n], pltpu.roll(p[n], ROWS - 1, 0)))
            q = q[8:136].T
            total = q[0:32] + q[32:64] + q[64:96] + bias3 + scaled[x + RIM, :, 0:128]
            out_ref[pl.ds(x, 32, stride=16), :] = total


def solution(mesh):
    nx, ny = mesh.shape["gx"], mesh.shape["gy"]

    def per_device(gradient, corr_length, scale, w_first, b_first, w_middle, b_middle, w_last, b_last):
        w1 = jnp.transpose(w_first, (2, 3, 4, 1, 0)).reshape(27, 2, 16)
        w2 = jnp.transpose(w_middle, (2, 3, 4, 0, 1)).reshape(432, 16)
        w3 = jnp.transpose(w_last, (2, 3, 4, 0, 1)).reshape(27, 2, 16)
        smem = pl.BlockSpec(memory_space=pltpu.SMEM)
        vmem = pl.BlockSpec(memory_space=pltpu.VMEM)

        def body(*refs):
            kernel(nx, ny, *refs)

        v = pltpu.VMEM
        out = pl.pallas_call(
            body,
            out_shape=jax.ShapeDtypeStruct((512, 128), F32),
            in_specs=[smem] * 4 + [vmem] * 5,
            out_specs=vmem,
            scratch_shapes=[
                v((2, 16, 16, 128), BF16), v((2, 6, 16, 128), BF16),
                v((2, HALO, 16, 128), BF16), v((2, HALO, 16, 128), BF16),
                v((2, RIM, 16, 128), BF16), v((2, RIM, 16, 128), BF16),
                v((54, 4, 8, 128), F32), v((24, 4, 8, 128), F32), v((24, 32, 128), F32),
                v((2, 6, 16, 128), F32), v((2, 6, 16, 128), F32), v((2, 6, 16, 128), F32), v((2, 6, 16, 128), F32),
                v((2, 128, 256), BF16), v((2, 128, 256), BF16),
                v((2, 4, 256, 384), BF16), v((2, 4, 256, 384), BF16), v((2, 16, 48), BF16),
                v((24, 32, 256), F32), v((24, 32, 256), F32),
                v((20, 160, 128), F32), v((20, ROWS, 384), BF16), v((20, ROWS, 768), BF16), v((18, ROWS, 256), BF16),
                v((384, 256), BF16), v((9, 256, 256), BF16), v((3, 256, 128), BF16), v((64, 16), F32), v((72, 16), F32),
                pltpu.SemaphoreType.DMA((12,)), pltpu.SemaphoreType.DMA((12,)),
                pltpu.SemaphoreType.DMA((4,)), pltpu.SemaphoreType.DMA((4,)),
            ],
            compiler_params=pltpu.CompilerParams(
                collective_id=0, has_side_effects=True, vmem_limit_bytes=56 * 1024 * 1024
            ),
        )(corr_length, b_first, b_middle, b_last, gradient.reshape(512, 128), scale.reshape(512, 128), w1, w2, w3)
        return out.reshape(gradient.shape)

    block = P(None, None, "gx", "gy")
    return jax.shard_map(
        per_device,
        mesh=mesh,
        in_specs=(block, P(), block, P(), P(), P(), P(), P(), P()),
        out_specs=block,
        check_vma=False,
    )
```

```python
import math

import jax
import jax.numpy as jnp
from jax import lax
from jax.experimental import pallas as pl
from jax.experimental.pallas import tpu as pltpu
from jax.sharding import PartitionSpec as P

RAD = 16
RIM = 3
HALO = RAD + RIM
MESH = pl.DeviceIdType.MESH
F32 = jnp.float32
BF16 = jnp.bfloat16
ROWS = 144
ROOT = math.sqrt(3.0)


def iota(shape, dim):
    return lax.broadcasted_iota(jnp.int32, shape, dim)


def dot(a, b):
    return lax.dot_general(a, b, (((1,), (0,)), ((), ())), preferred_element_type=F32)


def dot_rows(a, b):
    return lax.dot_general(a, b, (((0,), (0,)), ((), ())), preferred_element_type=F32)


def split(value):
    high = value.astype(BF16)
    return high, (value - high.astype(F32)).astype(BF16)


def tap(length, distance):
    s = (ROOT * distance.astype(F32)) / length
    return (1.0 + s) * jnp.exp(-s)


def tap_rows(length):
    rows = [tap(length, jnp.full((8, 128), r, jnp.int32)) for r in range(RAD + 1)]
    total = rows[0] * rows[0]
    for row in rows[1:]:
        total = total + 2.0 * (row * row)
    inverse = 1.0 / jnp.sqrt(total)
    return [row * inverse for row in rows], inverse


def silu(v):
    half = 0.5 * v
    return half + half * jnp.tanh(half)


def kernel(
    nx, ny, lens, b1s, b2s, b3s, g_hbm, s_hbm, w1, w2, w3, out_ref,
    gsend, ssend, xl, xr, sl, sr, field, along, scales, pack_l, pack_r, from_l, from_r,
    own_h, own_l, rim_h, rim_l, zmat, smooth, scaled, turned, lhs, hid1, hid2, t1, t2, t3, flat1, flat3,
    g_ref, s_ref, in_sem, send_sem, recv_sem, ysend_sem, yrecv_sem,
):
    gx = lax.axis_index("gx")
    gy = lax.axis_index("gy")
    at = lambda step: {"gx": lax.rem(gx + nx + step, nx)}

    take_g = pltpu.make_async_copy(g_hbm, g_ref, in_sem.at[0])
    take_s = pltpu.make_async_copy(s_hbm, s_ref, in_sem.at[1])
    take_g.start()
    take_s.start()

    barrier = pltpu.get_barrier_semaphore()
    for step in (-1, 1, -2, 2):
        pl.semaphore_signal(barrier, inc=1, device_id=at(step), device_id_type=MESH)

    for step in (1, ny - 1):
        pl.semaphore_signal(barrier, inc=1, device_id={"gy": lax.rem(gy + step, ny)}, device_id_type=MESH)
    take_g.wait()
    take_s.wait()
    for f in range(2):
        for x in range(16):
            gsend[f, x] = g_ref[pl.ds(f * 256 + x, 16, stride=16), :].astype(BF16)
        for n, x in enumerate((0, 1, 2, 13, 14, 15)):
            ssend[f, n] = s_ref[pl.ds(f * 256 + x, 16, stride=16), :].astype(BF16)
    pl.semaphore_wait(barrier, 6)

    def remote(src, dst, n, step):
        return pltpu.make_async_remote_copy(
            src_ref=src, dst_ref=dst, send_sem=send_sem.at[n], recv_sem=recv_sem.at[n],
            device_id=at(step), device_id_type=MESH,
        )

    copies = []
    for f in range(2):
        n = 6 * f
        copies.append([
            remote(gsend.at[f], xl.at[f, pl.ds(RIM, 16)], n, 1),
            remote(gsend.at[f], xr.at[f, pl.ds(0, 16)], n + 1, -1),
            remote(gsend.at[f, pl.ds(13, 3)], xl.at[f, pl.ds(0, RIM)], n + 2, 2),
            remote(gsend.at[f, pl.ds(0, 3)], xr.at[f, pl.ds(16, RIM)], n + 3, -2),
            remote(ssend.at[f, pl.ds(3, 3)], sl.at[f], n + 4, 1),
            remote(ssend.at[f, pl.ds(0, 3)], sr.at[f], n + 5, -1),
        ])
    for copy in copies[0] + copies[1]:
        copy.start()

    for x in range(16):
        field[HALO + x] = g_ref[pl.ds(x, 32, stride=16), :].reshape(4, 8, 128)
        scales[RIM + x] = s_ref[pl.ds(x, 32, stride=16), :]
    for x in (22, 23):
        scales[x] = jnp.zeros((32, 128), F32)
        along[x] = jnp.zeros((4, 8, 128), F32)
        scaled[x] = jnp.zeros((32, 256), F32)

    for x in range(20):
        turned[x, 0:16, :] = jnp.zeros((16, 128), F32)
        turned[x, 144:160, :] = jnp.zeros((16, 128), F32)

    pick = (iota((16, 256), 1) % 16 == iota((16, 256), 0)).astype(BF16)
    level = iota((16, 256), 1) // 16
    flat3[...] = jnp.zeros((72, 16), F32)
    for k in range(27):
        flat1[2 * k : 2 * k + 2, :] = w1[k].astype(F32)
        flat3[k // 3 * 8 + k % 3 * 2 : k // 3 * 8 + k % 3 * 2 + 2, :] = w3[k].astype(F32)
    wide1 = dot(flat1[...].astype(BF16), pick)
    row = iota((16, 256), 0)
    for dy in range(3):
        for dx in range(3):
            for f in range(2):
                block = jnp.zeros((16, 256), F32)
                for dz in range(3):
                    k = ((dz * 3 + dx) * 3 + dy) * 2 + f
                    block = jnp.where(level == row + 1 - dz, wide1[k : k + 1, :], block)
                t1[dy * 128 + dx * 32 + f * 16 : dy * 128 + dx * 32 + f * 16 + 16, :] = block.astype(BF16)
        t1[dy * 128 + 96 : dy * 128 + 128, :] = jnp.zeros((32, 256), BF16)

    def one_pair(n, carry):
        blocks = [dot_rows(w2[pl.ds(pl.multiple_of((dz * 9 + n) * 16, 16), 16), :], pick) for dz in range(3)]
        for zi in range(16):
            block = jnp.zeros((16, 256), F32)
            for dz in range(3):
                block = jnp.where(level == zi + 1 - dz, blocks[dz], block)
            t2[n, zi * 16 : zi * 16 + 16, :] = block.astype(BF16)
        return carry

    lax.fori_loop(0, 9, one_pair, 0)

    lane = iota((16, 128), 1)
    pick3 = ((iota((8, 128), 1) // 16 == iota((8, 128), 0)) & (iota((8, 128), 0) < 6)).astype(BF16)

    def one_shift(dx, carry):
        blocks = [dot_rows(flat3[pl.ds(pl.multiple_of((dz * 3 + dx) * 8, 8), 8), :].astype(BF16), pick3) for dz in range(3)]
        for zi in range(16):
            block = jnp.zeros((16, 128), F32)
            for dz in range(3):
                block = jnp.where((lane % 16 == zi + 1 - dz) & (lane < 96), blocks[dz], block)
            t3[dx, zi * 16 : zi * 16 + 16, :] = block.astype(BF16)
        return carry

    lax.fori_loop(0, 3, one_shift, 0)

    for f in range(2):
        length = lens[f, 1]
        inverse = tap_rows(length)[1][0:1, :]
        inverse2 = jnp.concatenate([inverse, inverse], axis=1)
        lanes = iota((128, 256), 1)
        target = jnp.where(lanes < 128, lanes, jnp.where(lanes < 131, lanes - 131, lanes - 3))
        away = jnp.abs(iota((128, 256), 0) - target)
        band = jnp.where((away <= RAD) & (lanes < 134), tap(length, away) * inverse2, 0.0)
        own_h[f], own_l[f] = split(band)

        def one_quarter(j, carry):
            for side in range(2):
                place = iota((128, 256), 0)
                k = place % 32
                source = k - HALO if side == 0 else k + 128
                away = jnp.abs(source - target)
                good = (place // 32 == j) & (k < HALO) & (away <= RAD) & (lanes < 134)
                band = jnp.where(good, tap(length, away) * inverse2, 0.0)
                high, low = split(band)
                rim_h[f, j, side * 128 : side * 128 + 128, 0:256] = high
                rim_l[f, j, side * 128 : side * 128 + 128, 0:256] = low
                place1 = iota((128, 128), 0)
                one = (place1 // 32 == j) & (place1 % 32 >= HALO) & (place1 % 32 < HALO + RIM)
                one = one & (iota((128, 128), 1) == place1 % 32 - HALO + RIM * side)
                rim_h[f, j, side * 128 : side * 128 + 128, 256:384] = one.astype(BF16)
                rim_l[f, j, side * 128 : side * 128 + 128, 256:384] = jnp.zeros((128, 128), BF16)
            return carry

        lax.fori_loop(0, 4, one_quarter, 0)

    away = jnp.abs(iota((16, 16), 0) - iota((16, 16), 1))
    for f in range(2):
        inverse = tap_rows(lens[f, 2])[1][0:1, 0:16]
        high, low = split(tap(lens[f, 2], away) * inverse)
        zmat[f] = jnp.concatenate([high, high, low], axis=1)

    def weighted(rows, f, x, kept):
        part = lambda k: field[x + k, 2 * f : 2 * f + 2]
        total = None
        for r in range(RAD + 1):
            taken = [part(k) for k in sorted({RAD - r, RAD + r}) if kept(x + k)]
            if taken:
                term = rows[r] * (taken[0] if len(taken) == 1 else taken[0] + taken[1])
                total = term if total is None else total + term
        return total

    mine = lambda row: HALO <= row < HALO + 16
    for f in range(2):
        rows = tap_rows(lens[f, 0])[0]
        for x in range(22):
            along[x, 2 * f : 2 * f + 2] = weighted(rows, f, x, mine)

    lane16 = iota((16, 128), 1)

    def edge(src, dst, n, to):
        return pltpu.make_async_remote_copy(
            src_ref=src, dst_ref=dst, send_sem=ysend_sem.at[n], recv_sem=yrecv_sem.at[n],
            device_id={"gy": to}, device_id_type=MESH,
        )

    to_right = [edge(pack_r.at[f], from_l.at[f], f, lax.rem(gy + 1, ny)) for f in range(2)]
    to_left = [edge(pack_l.at[f], from_r.at[f], 2 + f, lax.rem(gy + ny - 1, ny)) for f in range(2)]

    for f in range(2):
        for copy in copies[f]:
            copy.wait()
        for x in range(HALO):
            left_in = gx * 16 - HALO + x >= 0
            right_in = gx * 16 + 16 + x < nx * 16
            field[x, 2 * f : 2 * f + 2] = jnp.where(left_in, xl[f, x].astype(F32), 0.0).reshape(2, 8, 128)
            field[HALO + 16 + x, 2 * f : 2 * f + 2] = jnp.where(right_in, xr[f, x].astype(F32), 0.0).reshape(2, 8, 128)
        for x in range(RIM):
            scales[x, 16 * f : 16 * f + 16] = jnp.where(gx > 0, sl[f, x].astype(F32), 0.0)
            scales[RIM + 16 + x, 16 * f : 16 * f + 16] = jnp.where(gx < nx - 1, sr[f, x].astype(F32), 0.0)
        rows = tap_rows(lens[f, 0])[0]
        for x in range(22):
            along[x, 2 * f : 2 * f + 2] += weighted(rows, f, x, lambda row: not mine(row))

        for g in range(6):
            left = jnp.zeros((16, 128), F32)
            right = jnp.zeros((16, 128), F32)
            for j in range(4):
                a = along[4 * g + j, 2 * f : 2 * f + 2].reshape(16, 128)
                s = scales[4 * g + j, 16 * f : 16 * f + 16]
                inside = (lane16 >= 32 * j) & (lane16 < 32 * j + HALO)
                beside = (lane16 >= 32 * j + HALO) & (lane16 < 32 * j + HALO + RIM)
                right = jnp.where(inside, pltpu.roll(a, (32 * j + HALO) % 128, 1), right)
                right = jnp.where(beside, pltpu.roll(s, (32 * j + HALO + RIM) % 128, 1), right)
                left = jnp.where(inside, a if j == 0 else pltpu.roll(a, 32 * j, 1), left)
                left = jnp.where(beside, pltpu.roll(s, 32 * j + HALO, 1), left)
            pack_l[f, g] = left
            pack_r[f, g] = right

        @pl.when(gy < ny - 1)
        def _():
            to_right[f].start()

        @pl.when(gy > 0)
        def _():
            to_left[f].start()

        high, low = split(along[:, 2 * f : 2 * f + 2].reshape(384, 128))
        own = dot(high, own_h[f]) + dot(low, own_h[f]) + dot(high, own_l[f])
        smooth[:, f * 16 : f * 16 + 16, :] = own.reshape(24, 16, 256)

    for f in range(2):
        @pl.when(gy < ny - 1)
        def _():
            to_right[f].wait_send()
            to_left[f].wait_recv()

        @pl.when(gy > 0)
        def _():
            to_left[f].wait_send()
            to_right[f].wait_recv()

        edge_l = jnp.where(gy > 0, from_l[f], 0.0).reshape(96, 128)
        edge_r = jnp.where(gy < ny - 1, from_r[f], 0.0).reshape(96, 128)
        high, low = split(jnp.concatenate([edge_l, edge_r], axis=1))
        for j in range(4):
            rim = dot(high, rim_h[f, j]) + dot(low, rim_h[f, j]) + dot(high, rim_l[f, j])
            rim = rim.reshape(6, 16, 384)
            for g in range(6):
                x = 4 * g + j
                if x < 22:
                    part = slice(f * 16, f * 16 + 16)
                    high1, low1 = split(smooth[x, part, :] + rim[g, :, 0:256])
                    z = dot(zmat[f], jnp.concatenate([high1, low1, high1], axis=0))
                    scaled[x, part, 0:128] = z[:, 0:128] * scales[x, part]
                    scaled[x, part, 128:256] = z[:, 128:256] * rim[g, :, 256:384]

    def one_turn(x, carry):
        turned[x, 16:144, :] = scaled[pl.ds(x, 4), :, 0:128].reshape(128, 128).T
        rim = scaled[pl.ds(x, 4), :, 128:256].reshape(128, 128).T
        turned[x, 13:16, :] = rim[0:3]
        turned[x, 144:147, :] = rim[3:6]
        for dy in range(3):
            lhs[x, :, dy * 128 : dy * 128 + 128] = turned[x, 7 + dy : 7 + dy + ROWS, :].astype(BF16)
        return carry

    lax.fori_loop(0, 20, one_turn, 0, unroll=5)

    lane256 = iota((1, 256), 1) % 16
    bias1 = jnp.zeros((1, 256), F32)
    bias2 = jnp.zeros((1, 256), F32)
    for o in range(16):
        bias1 = jnp.where(lane256 == o, b1s[o], bias1)
        bias2 = jnp.where(lane256 == o, b2s[o], bias2)
    y = iota((ROWS, 256), 0) - 8 + gy * 128
    y_in = (y >= 0) & (y < ny * 128)

    def one_first(c, carry):
        v = dot(lhs[pl.ds(c * 4, 4)].reshape(4 * ROWS, 384), t1[...]) + bias1
        v = silu(v).reshape(4, ROWS, 256)
        for n in range(4):
            x = gx * 16 - 2 + c * 4 + n
            h = jnp.where(y_in & (x >= 0) & (x < nx * 16), v[n], 0.0)
            hid1[c * 4 + n, :, 0:256] = pltpu.roll(h, 1, 0).astype(BF16)
            hid1[c * 4 + n, :, 256:512] = h.astype(BF16)
            hid1[c * 4 + n, :, 512:768] = pltpu.roll(h, ROWS - 1, 0).astype(BF16)
        return carry

    lax.fori_loop(0, 5, one_first, 0, unroll=True)

    def one_middle(c, carry):
        v = bias2
        for dx in range(3):
            v = v + dot(hid1[pl.ds(c * 6 + dx, 6)].reshape(6 * ROWS, 768), t2[pl.ds(3 * dx, 3)].reshape(768, 256))
        v = silu(v).reshape(6, ROWS, 256)
        for n in range(6):
            x = gx * 16 - 1 + c * 6 + n
            hid2[c * 6 + n] = jnp.where(y_in & (x >= 0) & (x < nx * 16), v[n], 0.0).astype(BF16)
        return carry

    lax.fori_loop(0, 3, one_middle, 0, unroll=True)

    lane3 = iota((ROWS, 128), 1)
    bias3 = jnp.where(iota((32, 128), 0) < 16, b3s[0], b3s[1])
    for c in range(4):
        p = dot(hid2[c * 4 : c * 4 + 4].reshape(4 * ROWS, 256), t3[0])
        for dx in range(1, 3):
            p = p + dot(hid2[c * 4 + dx : c * 4 + dx + 4].reshape(4 * ROWS, 256), t3[dx])
        p = p.reshape(4, ROWS, 128)
        for n in range(4):
            x = c * 4 + n
            q = jnp.where(lane3 < 32, pltpu.roll(p[n], 1, 0), jnp.where(lane3 < 64, p[n], pltpu.roll(p[n], ROWS - 1, 0)))
            q = q[8:136].T
            total = q[0:32] + q[32:64] + q[64:96] + bias3 + scaled[x + RIM, :, 0:128]
            out_ref[pl.ds(x, 32, stride=16), :] = total


def solution(mesh):
    nx, ny = mesh.shape["gx"], mesh.shape["gy"]

    def per_device(gradient, corr_length, scale, w_first, b_first, w_middle, b_middle, w_last, b_last):
        w1 = jnp.transpose(w_first, (2, 3, 4, 1, 0)).reshape(27, 2, 16)
        w2 = jnp.transpose(w_middle, (2, 3, 4, 0, 1)).reshape(432, 16)
        w3 = jnp.transpose(w_last, (2, 3, 4, 0, 1)).reshape(27, 2, 16)
        smem = pl.BlockSpec(memory_space=pltpu.SMEM)
        vmem = pl.BlockSpec(memory_space=pltpu.VMEM)

        def body(*refs):
            kernel(nx, ny, *refs)

        v = pltpu.VMEM
        out = pl.pallas_call(
            body,
            out_shape=jax.ShapeDtypeStruct((512, 128), F32),
            in_specs=[smem] * 4 + [pl.BlockSpec(memory_space=pl.ANY)] * 2 + [vmem] * 3,
            out_specs=vmem,
            scratch_shapes=[
                v((2, 16, 16, 128), BF16), v((2, 6, 16, 128), BF16),
                v((2, HALO, 16, 128), BF16), v((2, HALO, 16, 128), BF16),
                v((2, RIM, 16, 128), BF16), v((2, RIM, 16, 128), BF16),
                v((54, 4, 8, 128), F32), v((24, 4, 8, 128), F32), v((24, 32, 128), F32),
                v((2, 6, 16, 128), F32), v((2, 6, 16, 128), F32), v((2, 6, 16, 128), F32), v((2, 6, 16, 128), F32),
                v((2, 128, 256), BF16), v((2, 128, 256), BF16),
                v((2, 4, 256, 384), BF16), v((2, 4, 256, 384), BF16), v((2, 16, 48), BF16),
                v((24, 32, 256), F32), v((24, 32, 256), F32),
                v((20, 160, 128), F32), v((20, ROWS, 384), BF16), v((20, ROWS, 768), BF16), v((18, ROWS, 256), BF16),
                v((384, 256), BF16), v((9, 256, 256), BF16), v((3, 256, 128), BF16), v((64, 16), F32), v((72, 16), F32),
                v((512, 128), F32), v((512, 128), F32), pltpu.SemaphoreType.DMA((2,)),
                pltpu.SemaphoreType.DMA((12,)), pltpu.SemaphoreType.DMA((12,)),
                pltpu.SemaphoreType.DMA((4,)), pltpu.SemaphoreType.DMA((4,)),
            ],
            compiler_params=pltpu.CompilerParams(
                collective_id=0, has_side_effects=True, vmem_limit_bytes=56 * 1024 * 1024
            ),
        )(corr_length, b_first, b_middle, b_last, gradient.reshape(512, 128), scale.reshape(512, 128), w1, w2, w3)
        return out.reshape(gradient.shape)

    block = P(None, None, "gx", "gy")
    return jax.shard_map(
        per_device,
        mesh=mesh,
        in_specs=(block, P(), block, P(), P(), P(), P(), P(), P()),
        out_specs=block,
        check_vma=False,
    )
```

```python
import math

import jax
import jax.numpy as jnp
from jax import lax
from jax.experimental import pallas as pl
from jax.experimental.pallas import tpu as pltpu
from jax.sharding import PartitionSpec as P

RAD = 16
RIM = 3
HALO = RAD + RIM
MESH = pl.DeviceIdType.MESH
F32 = jnp.float32
BF16 = jnp.bfloat16
ROWS = 144
ROOT = math.sqrt(3.0)


def iota(shape, dim):
    return lax.broadcasted_iota(jnp.int32, shape, dim)


def dot(a, b):
    return lax.dot_general(a, b, (((1,), (0,)), ((), ())), preferred_element_type=F32)


def dot_rows(a, b):
    return lax.dot_general(a, b, (((0,), (0,)), ((), ())), preferred_element_type=F32)


def split(value):
    high = value.astype(BF16)
    return high, (value - high.astype(F32)).astype(BF16)


def tap(length, distance):
    s = (ROOT * distance.astype(F32)) / length
    return (1.0 + s) * jnp.exp(-s)


def tap_rows(length):
    rows = [tap(length, jnp.full((8, 128), r, jnp.int32)) for r in range(RAD + 1)]
    total = rows[0] * rows[0]
    for row in rows[1:]:
        total = total + 2.0 * (row * row)
    inverse = 1.0 / jnp.sqrt(total)
    return [row * inverse for row in rows], inverse


def silu(v):
    half = 0.5 * v
    return half + half * jnp.tanh(half)


def kernel(
    nx, ny, lens, b1s, b2s, b3s, g_hbm, s_hbm, w1, w2, w3, out_ref,
    gsend, ssend, xl, xr, sl, sr, field, along, scales, pack_l, pack_r, from_l, from_r,
    own_h, own_l, rim_h, rim_l, zmat, smooth, scaled, turned, lhs, hid1, hid2, t1, t2, t3, flat1, flat3,
    g_ref, s_ref, in_sem, send_sem, recv_sem, ysend_sem, yrecv_sem,
):
    gx = lax.axis_index("gx")
    gy = lax.axis_index("gy")
    at = lambda step: {"gx": lax.rem(gx + nx + step, nx)}

    take_g = pltpu.make_async_copy(g_hbm, g_ref, in_sem.at[0])
    take_s = pltpu.make_async_copy(s_hbm, s_ref, in_sem.at[1])
    take_g.start()
    take_s.start()

    barrier = pltpu.get_barrier_semaphore()
    for step in (-1, 1, -2, 2):
        pl.semaphore_signal(barrier, inc=1, device_id=at(step), device_id_type=MESH)

    for step in (1, ny - 1):
        pl.semaphore_signal(barrier, inc=1, device_id={"gy": lax.rem(gy + step, ny)}, device_id_type=MESH)
    take_g.wait()
    take_s.wait()
    for f in range(2):
        for x in range(16):
            gsend[f, x] = g_ref[pl.ds(f * 256 + x, 16, stride=16), :].astype(BF16)
        for n, x in enumerate((0, 1, 2, 13, 14, 15)):
            ssend[f, n] = s_ref[pl.ds(f * 256 + x, 16, stride=16), :].astype(BF16)
    pl.semaphore_wait(barrier, 6)

    def remote(src, dst, n, step):
        return pltpu.make_async_remote_copy(
            src_ref=src, dst_ref=dst, send_sem=send_sem.at[n], recv_sem=recv_sem.at[n],
            device_id=at(step), device_id_type=MESH,
        )

    copies = []
    for f in range(2):
        n = 6 * f
        copies.append([
            remote(gsend.at[f], xl.at[f, pl.ds(RIM, 16)], n, 1),
            remote(gsend.at[f], xr.at[f, pl.ds(0, 16)], n + 1, -1),
            remote(gsend.at[f, pl.ds(13, 3)], xl.at[f, pl.ds(0, RIM)], n + 2, 2),
            remote(gsend.at[f, pl.ds(0, 3)], xr.at[f, pl.ds(16, RIM)], n + 3, -2),
            remote(ssend.at[f, pl.ds(3, 3)], sl.at[f], n + 4, 1),
            remote(ssend.at[f, pl.ds(0, 3)], sr.at[f], n + 5, -1),
        ])
    for copy in copies[0] + copies[1]:
        copy.start()

    for x in range(16):
        field[HALO + x] = g_ref[pl.ds(x, 32, stride=16), :].reshape(4, 8, 128)
        scales[RIM + x] = s_ref[pl.ds(x, 32, stride=16), :]
    for x in (22, 23):
        scales[x] = jnp.zeros((32, 128), F32)
        along[x] = jnp.zeros((4, 8, 128), F32)
        scaled[x] = jnp.zeros((32, 256), F32)

    for x in range(20):
        turned[x, 0:16, :] = jnp.zeros((16, 128), F32)
        turned[x, 144:160, :] = jnp.zeros((16, 128), F32)

    pick = (iota((16, 256), 1) % 16 == iota((16, 256), 0)).astype(BF16)
    level = iota((16, 256), 1) // 16
    flat3[...] = jnp.zeros((72, 16), F32)
    for k in range(27):
        flat1[2 * k : 2 * k + 2, :] = w1[k].astype(F32)
        flat3[k // 3 * 8 + k % 3 * 2 : k // 3 * 8 + k % 3 * 2 + 2, :] = w3[k].astype(F32)
    wide1 = dot(flat1[...].astype(BF16), pick)
    row = iota((16, 256), 0)
    for dy in range(3):
        for dx in range(3):
            for f in range(2):
                block = jnp.zeros((16, 256), F32)
                for dz in range(3):
                    k = ((dz * 3 + dx) * 3 + dy) * 2 + f
                    block = jnp.where(level == row + 1 - dz, wide1[k : k + 1, :], block)
                t1[dy * 128 + dx * 32 + f * 16 : dy * 128 + dx * 32 + f * 16 + 16, :] = block.astype(BF16)
        t1[dy * 128 + 96 : dy * 128 + 128, :] = jnp.zeros((32, 256), BF16)

    def one_pair(n, carry):
        blocks = [dot_rows(w2[pl.ds(pl.multiple_of((dz * 9 + n) * 16, 16), 16), :], pick) for dz in range(3)]
        for zi in range(16):
            block = jnp.zeros((16, 256), F32)
            for dz in range(3):
                block = jnp.where(level == zi + 1 - dz, blocks[dz], block)
            t2[n, zi * 16 : zi * 16 + 16, :] = block.astype(BF16)
        return carry

    lax.fori_loop(0, 9, one_pair, 0)

    lane = iota((16, 128), 1)
    pick3 = ((iota((8, 128), 1) // 16 == iota((8, 128), 0)) & (iota((8, 128), 0) < 6)).astype(BF16)

    def one_shift(dx, carry):
        blocks = [dot_rows(flat3[pl.ds(pl.multiple_of((dz * 3 + dx) * 8, 8), 8), :].astype(BF16), pick3) for dz in range(3)]
        for zi in range(16):
            block = jnp.zeros((16, 128), F32)
            for dz in range(3):
                block = jnp.where((lane % 16 == zi + 1 - dz) & (lane < 96), blocks[dz], block)
            t3[dx, zi * 16 : zi * 16 + 16, :] = block.astype(BF16)
        return carry

    lax.fori_loop(0, 3, one_shift, 0)

    for f in range(2):
        length = lens[f, 1]
        inverse = tap_rows(length)[1][0:1, :]
        inverse2 = jnp.concatenate([inverse, inverse], axis=1)
        lanes = iota((128, 256), 1)
        target = jnp.where(lanes < 128, lanes, jnp.where(lanes < 131, lanes - 131, lanes - 3))
        away = jnp.abs(iota((128, 256), 0) - target)
        band = jnp.where((away <= RAD) & (lanes < 134), tap(length, away) * inverse2, 0.0)
        own_h[f], own_l[f] = split(band)

        def one_quarter(j, carry):
            for side in range(2):
                place = iota((128, 256), 0)
                k = place % 32
                source = k - HALO if side == 0 else k + 128
                away = jnp.abs(source - target)
                good = (place // 32 == j) & (k < HALO) & (away <= RAD) & (lanes < 134)
                band = jnp.where(good, tap(length, away) * inverse2, 0.0)
                high, low = split(band)
                rim_h[f, j, side * 128 : side * 128 + 128, 0:256] = high
                rim_l[f, j, side * 128 : side * 128 + 128, 0:256] = low
                place1 = iota((128, 128), 0)
                one = (place1 // 32 == j) & (place1 % 32 >= HALO) & (place1 % 32 < HALO + RIM)
                one = one & (iota((128, 128), 1) == place1 % 32 - HALO + RIM * side)
                rim_h[f, j, side * 128 : side * 128 + 128, 256:384] = one.astype(BF16)
                rim_l[f, j, side * 128 : side * 128 + 128, 256:384] = jnp.zeros((128, 128), BF16)
            return carry

        lax.fori_loop(0, 4, one_quarter, 0)

    away = jnp.abs(iota((16, 16), 0) - iota((16, 16), 1))
    for f in range(2):
        inverse = tap_rows(lens[f, 2])[1][0:1, 0:16]
        high, low = split(tap(lens[f, 2], away) * inverse)
        zmat[f] = jnp.concatenate([high, high, low], axis=1)

    def weighted(rows, f, x, kept):
        part = lambda k: field[x + k, 2 * f : 2 * f + 2]
        total = None
        for r in range(RAD + 1):
            taken = [part(k) for k in sorted({RAD - r, RAD + r}) if kept(x + k)]
            if taken:
                term = rows[r] * (taken[0] if len(taken) == 1 else taken[0] + taken[1])
                total = term if total is None else total + term
        return total

    mine = lambda row: HALO <= row < HALO + 16
    for f in range(2):
        rows = tap_rows(lens[f, 0])[0]
        for x in range(22):
            along[x, 2 * f : 2 * f + 2] = weighted(rows, f, x, mine)

    lane16 = iota((16, 128), 1)

    def edge(src, dst, n, to):
        return pltpu.make_async_remote_copy(
            src_ref=src, dst_ref=dst, send_sem=ysend_sem.at[n], recv_sem=yrecv_sem.at[n],
            device_id={"gy": to}, device_id_type=MESH,
        )

    to_right = [edge(pack_r.at[f], from_l.at[f], f, lax.rem(gy + 1, ny)) for f in range(2)]
    to_left = [edge(pack_l.at[f], from_r.at[f], 2 + f, lax.rem(gy + ny - 1, ny)) for f in range(2)]

    for f in range(2):
        for copy in copies[f]:
            copy.wait()
        for x in range(HALO):
            left_in = gx * 16 - HALO + x >= 0
            right_in = gx * 16 + 16 + x < nx * 16
            field[x, 2 * f : 2 * f + 2] = jnp.where(left_in, xl[f, x].astype(F32), 0.0).reshape(2, 8, 128)
            field[HALO + 16 + x, 2 * f : 2 * f + 2] = jnp.where(right_in, xr[f, x].astype(F32), 0.0).reshape(2, 8, 128)
        for x in range(RIM):
            scales[x, 16 * f : 16 * f + 16] = jnp.where(gx > 0, sl[f, x].astype(F32), 0.0)
            scales[RIM + 16 + x, 16 * f : 16 * f + 16] = jnp.where(gx < nx - 1, sr[f, x].astype(F32), 0.0)
        rows = tap_rows(lens[f, 0])[0]
        for x in range(22):
            along[x, 2 * f : 2 * f + 2] += weighted(rows, f, x, lambda row: not mine(row))

        for g in range(6):
            left = jnp.zeros((16, 128), F32)
            right = jnp.zeros((16, 128), F32)
            for j in range(4):
                a = along[4 * g + j, 2 * f : 2 * f + 2].reshape(16, 128)
                s = scales[4 * g + j, 16 * f : 16 * f + 16]
                inside = (lane16 >= 32 * j) & (lane16 < 32 * j + HALO)
                beside = (lane16 >= 32 * j + HALO) & (lane16 < 32 * j + HALO + RIM)
                right = jnp.where(inside, pltpu.roll(a, (32 * j + HALO) % 128, 1), right)
                right = jnp.where(beside, pltpu.roll(s, (32 * j + HALO + RIM) % 128, 1), right)
                left = jnp.where(inside, a if j == 0 else pltpu.roll(a, 32 * j, 1), left)
                left = jnp.where(beside, pltpu.roll(s, 32 * j + HALO, 1), left)
            pack_l[f, g] = left
            pack_r[f, g] = right

        @pl.when(gy < ny - 1)
        def _():
            to_right[f].start()

        @pl.when(gy > 0)
        def _():
            to_left[f].start()

        high, low = split(along[:, 2 * f : 2 * f + 2].reshape(384, 128))
        own = dot(high, own_h[f]) + dot(low, own_h[f]) + dot(high, own_l[f])
        smooth[:, f * 16 : f * 16 + 16, :] = own.reshape(24, 16, 256)

    for f in range(2):
        @pl.when(gy < ny - 1)
        def _():
            to_right[f].wait_send()
            to_left[f].wait_recv()

        @pl.when(gy > 0)
        def _():
            to_left[f].wait_send()
            to_right[f].wait_recv()

        edge_l = jnp.where(gy > 0, from_l[f], 0.0).reshape(96, 128)
        edge_r = jnp.where(gy < ny - 1, from_r[f], 0.0).reshape(96, 128)
        high, low = split(jnp.concatenate([edge_l, edge_r], axis=1))
        for j in range(4):
            rim = dot(high, rim_h[f, j]) + dot(low, rim_h[f, j]) + dot(high, rim_l[f, j])
            rim = rim.reshape(6, 16, 384)
            for g in range(6):
                x = 4 * g + j
                if x < 22:
                    part = slice(f * 16, f * 16 + 16)
                    high1, low1 = split(smooth[x, part, :] + rim[g, :, 0:256])
                    z = dot(zmat[f], jnp.concatenate([high1, low1, high1], axis=0))
                    scaled[x, part, 0:128] = z[:, 0:128] * scales[x, part]
                    scaled[x, part, 128:256] = z[:, 128:256] * rim[g, :, 256:384]

    def one_turn(x, carry):
        turned[x, 16:144, :] = scaled[pl.ds(x, 4), :, 0:128].reshape(128, 128).T
        rim = scaled[pl.ds(x, 4), :, 128:256].reshape(128, 128).T
        turned[x, 13:16, :] = rim[0:3]
        turned[x, 144:147, :] = rim[3:6]
        for dy in range(3):
            lhs[x, :, dy * 128 : dy * 128 + 128] = turned[x, 7 + dy : 7 + dy + ROWS, :].astype(BF16)
        return carry

    for x in range(20):
        one_turn(x, 0)

    lane256 = iota((1, 256), 1) % 16
    bias1 = jnp.zeros((1, 256), F32)
    bias2 = jnp.zeros((1, 256), F32)
    for o in range(16):
        bias1 = jnp.where(lane256 == o, b1s[o], bias1)
        bias2 = jnp.where(lane256 == o, b2s[o], bias2)
    y = iota((ROWS, 256), 0) - 8 + gy * 128
    y_in = (y >= 0) & (y < ny * 128)

    def one_first(c, carry):
        v = dot(lhs[pl.ds(c * 4, 4)].reshape(4 * ROWS, 384), t1[...]) + bias1
        v = silu(v).reshape(4, ROWS, 256)
        for n in range(4):
            x = gx * 16 - 2 + c * 4 + n
            h = jnp.where(y_in & (x >= 0) & (x < nx * 16), v[n], 0.0)
            hid1[c * 4 + n, :, 0:256] = pltpu.roll(h, 1, 0).astype(BF16)
            hid1[c * 4 + n, :, 256:512] = h.astype(BF16)
            hid1[c * 4 + n, :, 512:768] = pltpu.roll(h, ROWS - 1, 0).astype(BF16)
        return carry

    for c in range(5):
        one_first(c, 0)

    def one_middle(c, carry):
        v = bias2
        for dx in range(3):
            v = v + dot(hid1[pl.ds(c * 3 + dx, 3)].reshape(3 * ROWS, 768), t2[pl.ds(3 * dx, 3)].reshape(768, 256))
        v = silu(v).reshape(3, ROWS, 256)
        for n in range(3):
            x = gx * 16 - 1 + c * 3 + n
            hid2[c * 3 + n] = jnp.where(y_in & (x >= 0) & (x < nx * 16), v[n], 0.0).astype(BF16)
        return carry

    for c in range(6):
        one_middle(c, 0)

    lane3 = iota((ROWS, 128), 1)
    bias3 = jnp.where(iota((32, 128), 0) < 16, b3s[0], b3s[1])
    for c in range(4):
        p = dot(hid2[c * 4 : c * 4 + 4].reshape(4 * ROWS, 256), t3[0])
        for dx in range(1, 3):
            p = p + dot(hid2[c * 4 + dx : c * 4 + dx + 4].reshape(4 * ROWS, 256), t3[dx])
        p = p.reshape(4, ROWS, 128)
        for n in range(4):
            x = c * 4 + n
            q = jnp.where(lane3 < 32, pltpu.roll(p[n], 1, 0), jnp.where(lane3 < 64, p[n], pltpu.roll(p[n], ROWS - 1, 0)))
            q = q[8:136].T
            total = q[0:32] + q[32:64] + q[64:96] + bias3 + scaled[x + RIM, :, 0:128]
            out_ref[pl.ds(x, 32, stride=16), :] = total


def solution(mesh):
    nx, ny = mesh.shape["gx"], mesh.shape["gy"]

    def per_device(gradient, corr_length, scale, w_first, b_first, w_middle, b_middle, w_last, b_last):
        w1 = jnp.transpose(w_first, (2, 3, 4, 1, 0)).reshape(27, 2, 16)
        w2 = jnp.transpose(w_middle, (2, 3, 4, 0, 1)).reshape(432, 16)
        w3 = jnp.transpose(w_last, (2, 3, 4, 0, 1)).reshape(27, 2, 16)
        smem = pl.BlockSpec(memory_space=pltpu.SMEM)
        vmem = pl.BlockSpec(memory_space=pltpu.VMEM)

        def body(*refs):
            kernel(nx, ny, *refs)

        v = pltpu.VMEM
        out = pl.pallas_call(
            body,
            out_shape=jax.ShapeDtypeStruct((512, 128), F32),
            in_specs=[smem] * 4 + [pl.BlockSpec(memory_space=pl.ANY)] * 2 + [vmem] * 3,
            out_specs=vmem,
            scratch_shapes=[
                v((2, 16, 16, 128), BF16), v((2, 6, 16, 128), BF16),
                v((2, HALO, 16, 128), BF16), v((2, HALO, 16, 128), BF16),
                v((2, RIM, 16, 128), BF16), v((2, RIM, 16, 128), BF16),
                v((54, 4, 8, 128), F32), v((24, 4, 8, 128), F32), v((24, 32, 128), F32),
                v((2, 6, 16, 128), F32), v((2, 6, 16, 128), F32), v((2, 6, 16, 128), F32), v((2, 6, 16, 128), F32),
                v((2, 128, 256), BF16), v((2, 128, 256), BF16),
                v((2, 4, 256, 384), BF16), v((2, 4, 256, 384), BF16), v((2, 16, 48), BF16),
                v((24, 32, 256), F32), v((24, 32, 256), F32),
                v((20, 160, 128), F32), v((20, ROWS, 384), BF16), v((20, ROWS, 768), BF16), v((18, ROWS, 256), BF16),
                v((384, 256), BF16), v((9, 256, 256), BF16), v((3, 256, 128), BF16), v((64, 16), F32), v((72, 16), F32),
                v((512, 128), F32), v((512, 128), F32), pltpu.SemaphoreType.DMA((2,)),
                pltpu.SemaphoreType.DMA((12,)), pltpu.SemaphoreType.DMA((12,)),
                pltpu.SemaphoreType.DMA((4,)), pltpu.SemaphoreType.DMA((4,)),
            ],
            compiler_params=pltpu.CompilerParams(
                collective_id=0, has_side_effects=True, vmem_limit_bytes=56 * 1024 * 1024
            ),
        )(corr_length, b_first, b_middle, b_last, gradient.reshape(512, 128), scale.reshape(512, 128), w1, w2, w3)
        return out.reshape(gradient.shape)

    block = P(None, None, "gx", "gy")
    return jax.shard_map(
        per_device,
        mesh=mesh,
        in_specs=(block, P(), block, P(), P(), P(), P(), P(), P()),
        out_specs=block,
        check_vma=False,
    )
```
